512 devices in a mesh: aux: 128 (over z, x_hi, y), occ: 4 (over x_lo, core).
Axes of the slice: x: 4 (x_hi: 2, x_lo: 2; x = x_hi * 2 + x_lo), y: 4, z: 16, core: 2. Of those that a mesh axis runs over, the one named last changes fastest.
Arguments:
- integrals: bfloat16 [2304, 32, 6144], P('aux', None, 'occ'), may hold values from -6 to 6
- coefficients: bfloat16 [6144, 48], P('occ'), may hold values from -0.29882812 to 0.29882812
- screening: int32 [32, 48], replicated, may hold values 0 or 1
- metric_factor: bfloat16 [2304, 2304], P('aux'), may hold values from -2 to 4
Outputs:
- gamma_block: bfloat16 [2304, 32, 6144], P('aux', 'occ')
The draws below stay inside these ranges and needn't reach their ends.
All inputs are finite; a program needn't handle non-finite values.
Results may differ from the reference program's by a relative error of at most 0.0057.
Values may be sent and summed in bfloat16 or wider, within the bound.
A program may use at most 64 MiB of HBM per device.

```python
import jax
import jax.numpy as jnp
from jax import lax

NBF = 6144
NOCC = 48
TILE = 128
AUXB = 2304
MU = 32


def draw_metric_factor(key, part):
    keyed = jax.random.fold_in(key, 7)
    first, second = jax.random.split(keyed)
    noise = jnp.clip(jax.random.normal(first, (AUXB, AUXB), jnp.float32), -3.0, 3.0)
    symmetric = (noise + noise.T) * (0.7071 / jnp.sqrt(jnp.float32(AUXB)))
    diagonal = jax.random.uniform(second, (AUXB,), jnp.float32, 1.0, 2.0)
    return (symmetric + jnp.diag(diagonal)).astype(jnp.bfloat16)


def with_ends(result, rng, smallest, high):
    spot = [jax.random.randint(jax.random.fold_in(rng, axis), (), 0, length) for axis, length in enumerate(result.shape)]
    longest = result.shape.index(max(result.shape))
    neighbour = spot[:longest] + [(spot[longest] + 1) % result.shape[longest]] + spot[longest + 1:]
    return result.at[tuple(spot)].set(smallest).at[tuple(neighbour)].set(high)


def level_of(own_key, dims, pieces, least, largest):
    loudness = 1.0
    for position, shards_of in pieces:
        heights = jax.random.uniform(jax.random.fold_in(jax.random.fold_in(own_key, 6), position), (shards_of,), jnp.float32, least / len(pieces), largest / len(pieces))
        loudness = loudness * jnp.repeat(jnp.exp(heights), dims[position] // shards_of).reshape((-1,) + (1,) * (len(dims) - 1 - position))
    return loudness


def scatter_about(key, extent, deviation, limit, shards=(), held_as=jnp.bfloat16):
    drawn = jax.random.normal(key, extent, jnp.float32) * deviation
    if len(shards) > 0:
        drawn = level_of(key, extent, shards, -0.22, 0.18) * drawn
    return jnp.clip(drawn, min=-limit, max=limit).astype(held_as)


def setup_inputs(seed: int = 0) -> dict:
    streams_of = jax.random.split(jax.random.key(seed), 5)
    integrals = scatter_about(streams_of[0], (AUXB, MU, NBF), 1.0, 6.0, ((0, 128), (2, 4)))
    coefficients = scatter_about(streams_of[1], (NBF, NOCC), 0.05, 0.29882812, ((0, 4),))
    screening = with_ends((jax.random.randint(streams_of[2], (MU, NBF // TILE), 0, 4) < 3).astype(jnp.int32), jax.random.fold_in(streams_of[2], 1), 0, 1)
    metric_factor = draw_metric_factor(jax.random.fold_in(streams_of[4], 71), 0)
    return dict(integrals=integrals, coefficients=coefficients, screening=screening, metric_factor=metric_factor)


def reference(integrals, coefficients, screening, metric_factor):
    screen = jnp.repeat(screening.astype(jnp.bfloat16), TILE, axis=1)

    def transform_one(integral_rows):
        masked = integral_rows * screen
        return jnp.dot(masked, coefficients, preferred_element_type=jnp.float32)

    half = lax.map(transform_one, integrals).astype(jnp.bfloat16)
    half_flat = half.reshape(AUXB, MU * NOCC)
    fitted = jnp.dot(metric_factor, half_flat, preferred_element_type=jnp.float32).astype(jnp.bfloat16)
    fitted_rows = fitted.reshape(AUXB, MU, NOCC)

    def gamma_one(fitted_one):
        product = lax.dot_general(fitted_one, coefficients, (((1,), (1,)), ((), ())), preferred_element_type=jnp.float32)
        return (product * screen.astype(jnp.float32)).astype(jnp.bfloat16)

    return lax.map(gamma_one, fitted_rows)
```

```python
import jax
import jax.numpy as jnp
from jax import lax
from jax.experimental import pallas as pl
from jax.experimental.pallas import tpu as pltpu
from jax.sharding import PartitionSpec as P

MESH = pl.DeviceIdType.MESH
BF = jnp.bfloat16
F32 = jnp.float32
TILE = 128

AUX = 18
ROWS = 32
MU = 8
OCC = 48
NU = 1536
NBF = 6144
LANES = 128
CHUNKS = 3
R = 64
PIECE = 16 * AUX
PIECE_PAD = 384
PIECE_ROWS = 32
STEPS = 3
STEP_AUX = AUX // STEPS
STEP_ROWS = STEP_AUX * ROWS


def iota(shape, dim):
    return lax.broadcasted_iota(jnp.int32, shape, dim)


def one_hot(cond):
    return jnp.where(cond, 1.0, 0.0).astype(F32).astype(BF)


def nn(a, b):
    return jnp.dot(a, b, preferred_element_type=F32)


def nt(a, b):
    return lax.dot_general(a, b, (((1,), (1,)), ((), ())), preferred_element_type=F32)


def transform_kernel(
    integrals, coef_t, screening, metric,
    fitted_out, coef_out, screen_out,
    ints, coef, mets, pieces, spread, parts, sends, recv1, half, halves, mrecv, mexp, fsend, recv3, fit,
    load_sem, coef_send, coef_recv, msend, mrecv_sem, send1, recv1_sem, send2, recv2_sem, send3, recv3_sem,
):
    aux = lax.axis_index("aux")
    occ = lax.axis_index("occ")
    z, xh, y = aux // 8, (aux // 4) % 2, aux % 4
    xl, core = occ // 2, occ % 2
    upper = z % 2
    sign = 2 * upper - 1
    place = upper * 8 + xh * 4 + y

    def at_z(distance):
        other = lax.rem(z + distance + 16, 16)
        return {"aux": other * 8 + xh * 4 + y, "occ": occ}

    def mate(k):
        other = lax.rem(xl + k // 2, 2) * 2 + lax.rem(core + k % 2, 2)
        return other

    def near(k):
        zp, xx, yy = lax.rem(upper + k // 8, 2), lax.rem(xh + (k // 4) % 2, 2), lax.rem(y + k % 4, 4)
        return (z - upper + zp) * 8 + xx * 4 + yy, zp * 8 + xx * 4 + yy

    def near_from(k):
        zp, xx, yy = lax.rem(upper + k // 8, 2), lax.rem(xh + (k // 4) % 2, 2), lax.rem(y + 4 - k % 4, 4)
        return (z - upper + zp) * 8 + xx * 4 + yy, zp * 8 + xx * 4 + yy

    barrier = pltpu.get_barrier_semaphore()
    for k in range(1, 4):
        pl.semaphore_signal(barrier, inc=1, device_id={"aux": aux, "occ": mate(k)}, device_id_type=MESH)
    for k in range(1, 16):
        pl.semaphore_signal(barrier, inc=1, device_id={"aux": near_from(k)[0], "occ": occ}, device_id_type=MESH)
    for d in range(1, 8):
        pl.semaphore_signal(barrier, inc=1, device_id=at_z(sign * d), device_id_type=MESH)
    for d in range(2, 8, 2):
        pl.semaphore_signal(barrier, inc=1, device_id=at_z(-sign * d), device_id_type=MESH)

    loads = [pltpu.make_async_copy(coef_t, coef, load_sem.at[STEPS])]
    for j in range(STEPS):
        loads.append(pltpu.make_async_copy(
            integrals.at[pl.ds(j * STEP_AUX, STEP_AUX)], ints.at[pl.ds(j * STEP_AUX, STEP_AUX)], load_sem.at[j]))
    loads.append(pltpu.make_async_copy(metric, mets, load_sem.at[STEPS + 1]))
    for copy in loads:
        copy.start()

    screen = screening[...].astype(F32).astype(BF)
    own_tile = iota((48, NU), 0) == occ * (NU // TILE) + iota((48, NU), 1) // TILE
    mask = nn(screen, one_hot(own_tile)).astype(BF)
    widen = one_hot(iota((OCC, CHUNKS * LANES), 0) == iota((OCC, CHUNKS * LANES), 1) % OCC)
    keep = (iota((ROWS, CHUNKS * LANES), 0) % MU) == (iota((ROWS, CHUNKS * LANES), 1) // OCC)
    keep = jnp.tile(jnp.where(keep, 1.0, 0.0).astype(F32), (STEP_AUX, 1))
    row = iota((4 * R, 1), 0)
    col = iota((1, AUX * ROWS), 1) // MU
    for c in range(CHUNKS):
        p = row % R - AUX * c
        wanted = jnp.where((p >= 0) & (p < AUX), p * 4 + row // R, -1)
        spread[:, c * AUX * ROWS:(c + 1) * AUX * ROWS] = one_hot(wanted == col)
    own_rows = one_hot(iota((16, ROWS), 1) == occ * MU + iota((16, ROWS), 0))
    screen_out[...] = nn(own_rows, screen).astype(BF)

    loads[-1].wait()
    pieces[...] = jnp.zeros_like(pieces)
    for k in range(8):
        pieces[k, 0:AUX, 0:PIECE] = mets[:, k * PIECE:(k + 1) * PIECE]

    loads[0].wait()
    for j in range(STEPS):
        loads[1 + j].wait()
        block = ints[j * STEP_AUX:(j + 1) * STEP_AUX] * mask[None]
        value = nt(block.reshape(STEP_ROWS, NU), coef[...]).astype(BF)
        wide = (nn(value, widen) * keep).astype(BF)
        for c in range(CHUNKS):
            lo = c * AUX * ROWS + j * STEP_ROWS
            parts[lo:lo + STEP_ROWS, :] = wide[:, c * LANES:(c + 1) * LANES]
    sends[...] = nn(spread[...], parts[...]).astype(BF).reshape(4, R, LANES)

    pl.semaphore_wait(barrier, 28)

    first = []
    for k in (3, 2, 1):
        copy = pltpu.make_async_remote_copy(
            src_ref=sends.at[mate(k)], dst_ref=recv1.at[k - 1], send_sem=send1.at[k - 1], recv_sem=recv1_sem.at[k - 1],
            device_id={"aux": aux, "occ": mate(k)}, device_id_type=MESH)
        copy.start()
        first.append(copy)
    metric_copies = []
    for d in (7, 6, 5, 4, 3, 2, 1):
        step = sign * d if d % 2 else -sign * d
        other = lax.rem(z + step + 16, 16)
        copy = pltpu.make_async_remote_copy(
            src_ref=pieces.at[other // 2], dst_ref=mrecv.at[d], send_sem=msend.at[d - 1], recv_sem=mrecv_sem.at[d - 1],
            device_id=at_z(step), device_id_type=MESH)
        copy.start()
        metric_copies.append(copy)
    mrecv[0] = pieces[z // 2]
    for copy in first:
        copy.wait_recv()
    total = sends[occ].astype(F32) + recv1[0].astype(F32) + recv1[1].astype(F32) + recv1[2].astype(F32)
    half[...] = total.astype(BF)

    second = []
    for k in (14, 15, 13, 10, 6, 11, 9, 7, 5, 2, 12, 3, 1, 8, 4):
        copy = pltpu.make_async_remote_copy(
            src_ref=half, dst_ref=halves.at[place], send_sem=send2.at[k - 1], recv_sem=recv2_sem.at[k - 1],
            device_id={"aux": near(k)[0], "occ": occ}, device_id_type=MESH)
        copy.start()
        second.append(copy)
    halves[place] = half[...]

    coef_copies = []
    for k in (3, 2, 1):
        copy = pltpu.make_async_remote_copy(
            src_ref=coef_t, dst_ref=coef_out.at[:, pl.ds(pl.multiple_of(occ * NU, NU), NU)],
            send_sem=coef_send.at[k - 1], recv_sem=coef_recv.at[k - 1],
            device_id={"aux": aux, "occ": mate(k)}, device_id_type=MESH)
        copy.start()
        coef_copies.append(copy)
    own_coef = pltpu.make_async_copy(coef, coef_out.at[:, pl.ds(pl.multiple_of(occ * NU, NU), NU)], load_sem.at[0])
    own_coef.start()

    for copy in metric_copies:
        copy.wait_recv()
    c_of_col = iota((PIECE_PAD, 16 * R), 1) % R
    source = (iota((PIECE_PAD, 16 * R), 1) // R) * AUX + c_of_col % AUX
    columns = one_hot((iota((PIECE_PAD, 16 * R), 0) == source) & (c_of_col < CHUNKS * AUX))
    wide_metric = nn(mrecv[...].reshape(8 * PIECE_ROWS, PIECE_PAD), columns).astype(BF)
    r_of_row = iota((8 * R, 1), 0) % R
    source = jnp.where(r_of_row < CHUNKS * AUX, (iota((8 * R, 1), 0) // R) * PIECE_ROWS + r_of_row % AUX, -1)
    rows = one_hot(source == iota((1, 8 * PIECE_ROWS), 1))
    same = (r_of_row // AUX) == ((iota((1, 16 * R), 1) % R) // AUX)
    mexp[...] = jnp.where(same, nn(rows, wide_metric), 0.0).astype(BF)

    for copy in second:
        copy.wait_recv()
    partial = nn(mexp[...], halves[...].reshape(16 * R, LANES)).reshape(8, R, LANES)
    fit[...] = partial[0]
    fsend[...] = partial.astype(BF)

    third = []
    for d in (7, 6, 5, 4, 3, 2, 1):
        copy = pltpu.make_async_remote_copy(
            src_ref=fsend.at[d], dst_ref=recv3.at[d - 1], send_sem=send3.at[d - 1], recv_sem=recv3_sem.at[d - 1],
            device_id=at_z(sign * d), device_id_type=MESH)
        copy.start()
        third.append(copy)
    for copy in third[::-1]:
        copy.wait_recv()
    total = fit[...]
    for d in range(7):
        total = total + recv3[d].astype(F32)
    fitted = total.astype(BF)

    wide_rows = iota((AUX * MU, R), 0)
    out = None
    for c in range(CHUNKS):
        pick = one_hot(iota((AUX * MU, R), 1) == wide_rows // MU + c * AUX)
        value = nn(pick, fitted)
        lane = iota((AUX * MU, LANES), 1) + c * LANES
        value = jnp.where(lane // OCC == iota((AUX * MU, LANES), 0) % MU, value, 0.0).astype(BF)
        fold = one_hot((iota((LANES, LANES), 0) + c * LANES) % OCC == iota((LANES, LANES), 1))
        value = nn(value, fold)
        out = value if out is None else out + value
    fitted_out[...] = out.astype(BF)

    own_coef.wait()
    for copy in coef_copies:
        copy.wait_recv()
    for copy in first + metric_copies + second + coef_copies + third:
        copy.wait_send()


def gamma_kernel(fitted, coef, screen, out):
    width = out.shape[2]
    tile = pl.program_id(0) * (width // TILE) + iota((48, width), 1) // TILE
    mask = nn(screen[...], one_hot(iota((48, width), 0) == tile))[0:MU]
    product = nn(fitted[...][:, 0:OCC], coef[...])
    out[...] = (product.reshape(AUX, MU, width) * mask[None]).astype(BF)


def on_device(integrals, coefficients, screening, metric_factor):
    hbm = pl.BlockSpec(memory_space=pl.ANY)
    vmem = pl.BlockSpec(memory_space=pltpu.VMEM)
    dma = pltpu.SemaphoreType.DMA
    fitted, coef_all, own_screen = pl.pallas_call(
        transform_kernel,
        name="exchange",
        out_shape=(
            jax.ShapeDtypeStruct((AUX * MU, LANES), BF),
            jax.ShapeDtypeStruct((OCC, NBF), BF),
            jax.ShapeDtypeStruct((16, 48), BF),
        ),
        in_specs=[hbm, hbm, vmem, hbm],
        out_specs=(vmem, hbm, vmem),
        scratch_shapes=[
            pltpu.VMEM((AUX, ROWS, NU), BF),
            pltpu.VMEM((OCC, NU), BF),
            pltpu.VMEM((AUX, 2304), BF),
            pltpu.VMEM((8, PIECE_ROWS, PIECE_PAD), BF),
            pltpu.VMEM((4 * R, CHUNKS * AUX * ROWS), BF),
            pltpu.VMEM((CHUNKS * AUX * ROWS, LANES), BF),
            pltpu.VMEM((4, R, LANES), BF),
            pltpu.VMEM((3, R, LANES), BF),
            pltpu.VMEM((R, LANES), BF),
            pltpu.VMEM((16, R, LANES), BF),
            pltpu.VMEM((8, PIECE_ROWS, PIECE_PAD), BF),
            pltpu.VMEM((8 * R, 16 * R), BF),
            pltpu.VMEM((8, R, LANES), BF),
            pltpu.VMEM((7, R, LANES), BF),
            pltpu.VMEM((R, LANES), F32),
            dma((STEPS + 2,)),
            dma((3,)), dma((3,)),
            dma((7,)), dma((7,)),
            dma((3,)), dma((3,)),
            dma((15,)), dma((15,)),
            dma((7,)), dma((7,)),
        ],
        compiler_params=pltpu.CompilerParams(collective_id=0, has_side_effects=True),
    )(integrals, coefficients.T, screening, metric_factor)
    width = 1024
    return pl.pallas_call(
        gamma_kernel,
        name="gamma",
        grid=(NBF // width,),
        out_shape=jax.ShapeDtypeStruct((AUX, MU, NBF), BF),
        in_specs=[
            pl.BlockSpec((AUX * MU, LANES), lambda j: (0, 0)),
            pl.BlockSpec((OCC, width), lambda j: (0, j)),
            pl.BlockSpec((16, 48), lambda j: (0, 0)),
        ],
        out_specs=pl.BlockSpec((AUX, MU, width), lambda j: (0, 0, j)),
    )(fitted, coef_all, own_screen)


def solution(mesh):
    return jax.shard_map(
        on_device,
        mesh=mesh,
        in_specs=(P("aux", None, "occ"), P("occ", None), P(), P("aux", None)),
        out_specs=P("aux", "occ", None),
        check_vma=False,
    )
```

```python
import jax
import jax.numpy as jnp
from jax import lax
from jax.experimental import pallas as pl
from jax.experimental.pallas import tpu as pltpu
from jax.sharding import PartitionSpec as P

MESH = pl.DeviceIdType.MESH
BF = jnp.bfloat16
F32 = jnp.float32
TILE = 128

AUX = 18
ROWS = 32
MU = 8
OCC = 48
NU = 1536
NBF = 6144
LANES = 128
CHUNKS = 3
R = 56
PIECE = 16 * AUX
PIECE_PAD = 384
PIECE_ROWS = 24
STEPS = 3
STEP_AUX = AUX // STEPS
STEP_ROWS = STEP_AUX * ROWS
GAMMA_STEPS = 6
EARLY = (7, 6, 5, 4, 3, 2, 1)
LATE = ()


def iota(shape, dim):
    return lax.broadcasted_iota(jnp.int32, shape, dim)


def one_hot(cond):
    return jnp.where(cond, 1.0, 0.0).astype(F32).astype(BF)


def nn(a, b):
    return jnp.dot(a, b, preferred_element_type=F32)


def nt(a, b):
    return lax.dot_general(a, b, (((1,), (1,)), ((), ())), preferred_element_type=F32)


def exchange_kernel(
    integrals, coef_t, screening, metric,
    fitted_out, coef_out, mask_out,
    ints, coef, mets, scr, pieces, spread, parts, sends, recv1, half, halves, mrecv, columns, rows, mexp, fsend, recv3, fit, pick, lanes, fold,
    load_sem, coef_send, coef_recv, msend, mrecv_sem, send1, recv1_sem, send2, recv2_sem, send3, recv3_sem,
):
    aux = lax.axis_index("aux")
    occ = lax.axis_index("occ")
    z, xh, y = aux // 8, (aux // 4) % 2, aux % 4
    xl, core = occ // 2, occ % 2
    upper = z % 2
    sign = 2 * upper - 1
    place = upper * 8 + xh * 4 + y

    def at_z(distance):
        other = lax.rem(z + distance + 16, 16)
        return {"aux": other * 8 + xh * 4 + y, "occ": occ}

    def mate(k):
        return lax.rem(xl + k // 2, 2) * 2 + lax.rem(core + k % 2, 2)

    def near(k, way):
        zp, xx, yy = lax.rem(upper + k // 8, 2), lax.rem(xh + (k // 4) % 2, 2), lax.rem(y + 4 + way * (k % 4), 4)
        return {"aux": (z - upper + zp) * 8 + xx * 4 + yy, "occ": occ}

    loads = [pltpu.make_async_copy(screening, scr, load_sem.at[0]), pltpu.make_async_copy(coef_t, coef, load_sem.at[1])]
    for j in range(STEPS):
        part = pl.ds(j * STEP_AUX, STEP_AUX)
        loads.append(pltpu.make_async_copy(integrals.at[part], ints.at[part], load_sem.at[2 + j]))
    loads.append(pltpu.make_async_copy(metric, mets, load_sem.at[2 + STEPS]))
    for copy in loads:
        copy.start()

    barrier = pltpu.get_barrier_semaphore()
    for k in range(1, 4):
        pl.semaphore_signal(barrier, inc=1, device_id={"aux": aux, "occ": mate(k)}, device_id_type=MESH)
    for k in range(1, 16):
        pl.semaphore_signal(barrier, inc=1, device_id=near(k, -1), device_id_type=MESH)
    for d in range(1, 8):
        pl.semaphore_signal(barrier, inc=1, device_id=at_z(sign * d), device_id_type=MESH)
    for d in range(2, 8, 2):
        pl.semaphore_signal(barrier, inc=1, device_id=at_z(-sign * d), device_id_type=MESH)

    widen = one_hot(iota((OCC, CHUNKS * LANES), 0) == iota((OCC, CHUNKS * LANES), 1) % OCC)
    keep = (iota((ROWS, CHUNKS * LANES), 0) % MU) == (iota((ROWS, CHUNKS * LANES), 1) // OCC)
    keep = jnp.tile(jnp.where(keep, 1.0, 0.0).astype(F32), (STEP_AUX, 1))
    row = iota((4 * R, 1), 0)
    col = iota((1, AUX * ROWS), 1) // MU
    for c in range(CHUNKS):
        p = row % R - AUX * c
        wanted = jnp.where((p >= 0) & (p < AUX), p * 4 + row // R, -1)
        spread[:, c * AUX * ROWS:(c + 1) * AUX * ROWS] = one_hot(wanted == col)
    own_tile = one_hot(iota((48, NU), 0) == occ * (NU // TILE) + iota((48, NU), 1) // TILE)
    loads[0].wait()
    screen = scr[...].astype(F32).astype(BF)
    mask = nn(screen, own_tile).astype(BF)

    loads[1].wait()
    for j in range(STEPS):
        loads[2 + j].wait()
        block = ints[j * STEP_AUX:(j + 1) * STEP_AUX] * mask[None]
        value = nt(block.reshape(STEP_ROWS, NU), coef[...]).astype(BF)
        wide = (nn(value, widen) * keep).astype(BF)
        for c in range(CHUNKS):
            lo = c * AUX * ROWS + j * STEP_ROWS
            parts[lo:lo + STEP_ROWS, :] = wide[:, c * LANES:(c + 1) * LANES]
    sends[...] = nn(spread[...], parts[...]).astype(BF).reshape(4, R, LANES)

    pl.semaphore_wait(barrier, 28)

    first = []
    for k in (3, 2, 1):
        copy = pltpu.make_async_remote_copy(
            src_ref=sends.at[mate(k)], dst_ref=recv1.at[k - 1], send_sem=send1.at[k - 1], recv_sem=recv1_sem.at[k - 1],
            device_id={"aux": aux, "occ": mate(k)}, device_id_type=MESH)
        copy.start()
        first.append(copy)

    loads[-1].wait()
    pieces[...] = jnp.zeros_like(pieces)
    for k in range(8):
        pieces[k, 0:AUX, 0:PIECE] = mets[:, k * PIECE:(k + 1) * PIECE]

    def send_metric(d):
        step = sign * d if d % 2 else -sign * d
        other = lax.rem(z + step + 16, 16)
        copy = pltpu.make_async_remote_copy(
            src_ref=pieces.at[other // 2], dst_ref=mrecv.at[d], send_sem=msend.at[d - 1], recv_sem=mrecv_sem.at[d - 1],
            device_id=at_z(step), device_id_type=MESH)
        copy.start()
        return copy

    metric_copies = [send_metric(d) for d in EARLY]
    mrecv[0] = pieces[z // 2]
    for copy in first:
        copy.wait_recv()
    total = sends[occ].astype(F32) + recv1[0].astype(F32) + recv1[1].astype(F32) + recv1[2].astype(F32)
    half[...] = total.astype(BF)

    second = []
    for k in (14, 13, 15, 6, 10, 12, 5, 7, 9, 11, 2, 4, 1, 3, 8):
        copy = pltpu.make_async_remote_copy(
            src_ref=half, dst_ref=halves.at[place], send_sem=send2.at[k - 1], recv_sem=recv2_sem.at[k - 1],
            device_id=near(k, 1), device_id_type=MESH)
        copy.start()
        second.append(copy)
    metric_copies += [send_metric(d) for d in LATE]
    halves[place] = half[...]

    own_nu = pl.ds(pl.multiple_of(occ * NU, NU), NU)
    to_core = pltpu.make_async_remote_copy(
        src_ref=coef_t, dst_ref=coef_out.at[:, own_nu], send_sem=coef_send.at[0], recv_sem=coef_recv.at[0],
        device_id={"aux": aux, "occ": mate(1)}, device_id_type=MESH)
    to_core.start()
    to_chip = pltpu.make_async_remote_copy(
        src_ref=coef_t, dst_ref=coef_out.at[:, own_nu], send_sem=coef_send.at[1], recv_sem=coef_recv.at[1],
        device_id={"aux": aux, "occ": mate(2)}, device_id_type=MESH)
    to_chip.start()
    own_coef = pltpu.make_async_copy(coef, coef_out.at[:, own_nu], load_sem.at[0])
    own_coef.start()

    c_of_col = iota((PIECE_PAD, 16 * R), 1) % R
    source = (iota((PIECE_PAD, 16 * R), 1) // R) * AUX + c_of_col % AUX
    columns[...] = one_hot((iota((PIECE_PAD, 16 * R), 0) == source) & (c_of_col < CHUNKS * AUX))
    r_of_row = iota((8 * R, 1), 0) % R
    source = jnp.where(r_of_row < CHUNKS * AUX, (iota((8 * R, 1), 0) // R) * PIECE_ROWS + r_of_row % AUX, -1)
    rows[...] = one_hot(source == iota((1, 8 * PIECE_ROWS), 1))
    row = iota((AUX * MU, 1), 0)
    for c in range(CHUNKS):
        pick[c * AUX * MU:(c + 1) * AUX * MU, :] = one_hot(iota((1, R), 1) == row // MU + c * AUX)
        lanes[c * AUX * MU:(c + 1) * AUX * MU, :] = jnp.where(
            (iota((1, LANES), 1) + c * LANES) // OCC == row % MU, 1.0, 0.0).astype(F32)
    fold[...] = one_hot(iota((CHUNKS * LANES, OCC), 0) % OCC == iota((CHUNKS * LANES, OCC), 1))
    own_rows = one_hot(iota((16, ROWS), 1) == occ * MU + iota((16, ROWS), 0) % MU)
    own_screen = nn(own_rows, screen).astype(BF)
    for k in range(4):
        tile = one_hot(iota((48, NU), 0) == k * (NU // TILE) + iota((48, NU), 1) // TILE)
        mask_out[:, k * NU:(k + 1) * NU] = nn(own_screen, tile)[0:MU]

    for copy in metric_copies:
        copy.wait_recv()
    wide_metric = nn(mrecv[...].reshape(8 * PIECE_ROWS, PIECE_PAD), columns[...]).astype(BF)
    same = ((iota((8 * R, 1), 0) % R) // AUX) == ((iota((1, 16 * R), 1) % R) // AUX)
    mexp[...] = jnp.where(same, nn(rows[...], wide_metric), 0.0).astype(BF)

    for copy in second:
        copy.wait_recv()
    partial = nn(mexp[...], halves[...].reshape(16 * R, LANES)).reshape(8, R, LANES)
    fsend[...] = partial.astype(BF)

    third = []
    for d in (7, 6, 5, 4, 3, 2, 1):
        copy = pltpu.make_async_remote_copy(
            src_ref=fsend.at[d], dst_ref=recv3.at[d - 1], send_sem=send3.at[d - 1], recv_sem=recv3_sem.at[d - 1],
            device_id=at_z(sign * d), device_id_type=MESH)
        copy.start()
        third.append(copy)
    fit[...] = partial[0]

    to_chip.wait_recv()
    chip_nu = pl.ds(pl.multiple_of(mate(2) * NU, NU), NU)
    onward = pltpu.make_async_remote_copy(
        src_ref=coef_out.at[:, chip_nu], dst_ref=coef_out.at[:, chip_nu], send_sem=coef_send.at[2], recv_sem=coef_recv.at[2],
        device_id={"aux": aux, "occ": mate(1)}, device_id_type=MESH)
    onward.start()

    total = fit[...]
    for d in range(1, 8):
        third[7 - d].wait_recv()
        total = total + recv3[d - 1].astype(F32)

    value = (nn(pick[...], total.astype(BF)) * lanes[...]).astype(BF)
    value = jnp.concatenate([value[c * AUX * MU:(c + 1) * AUX * MU] for c in range(CHUNKS)], axis=1)
    fitted_out[...] = nn(value, fold[...]).astype(BF)

    own_coef.wait()
    to_core.wait_recv()
    onward.wait_recv()
    for copy in first + metric_copies + second + third + [to_core, to_chip, onward]:
        copy.wait_send()


def gamma_kernel(fitted, coef, mask, out, buffer, sems):
    width = NBF // sems.shape[0]
    copies = []
    for k in range(sems.shape[0]):
        part = pl.ds(k * width, width)
        product = nn(fitted[...], coef[:, k * width:(k + 1) * width])
        scaled = product.reshape(AUX, MU, width) * mask[:, k * width:(k + 1) * width][None]
        buffer[:, k * width:(k + 1) * width] = scaled.reshape(AUX * MU, width).astype(BF)
        copies.append(pltpu.make_async_copy(buffer.at[:, part], out.at[:, part], sems.at[k]))
        copies[-1].start()
    for copy in copies:
        copy.wait()


def on_device(integrals, coefficients, screening, metric_factor):
    hbm = pl.BlockSpec(memory_space=pltpu.HBM)
    free = pl.BlockSpec(memory_space=pl.ANY)
    vmem = pl.BlockSpec(memory_space=pltpu.VMEM)
    dma = pltpu.SemaphoreType.DMA
    fitted, coef_all, mask = pl.pallas_call(
        exchange_kernel,
        name="exchange",
        out_shape=(
            jax.ShapeDtypeStruct((AUX * MU, OCC), BF),
            jax.ShapeDtypeStruct((OCC, NBF), BF),
            jax.ShapeDtypeStruct((MU, NBF), F32),
        ),
        in_specs=[hbm, hbm, hbm, hbm],
        out_specs=(vmem, free, vmem),
        scratch_shapes=[
            pltpu.VMEM((AUX, ROWS, NU), BF),
            pltpu.VMEM((OCC, NU), BF),
            pltpu.VMEM((AUX, 2304), BF),
            pltpu.VMEM((ROWS, 48), jnp.int32),
            pltpu.VMEM((8, PIECE_ROWS, PIECE_PAD), BF),
            pltpu.VMEM((4 * R, CHUNKS * AUX * ROWS), BF),
            pltpu.VMEM((CHUNKS * AUX * ROWS, LANES), BF),
            pltpu.VMEM((4, R, LANES), BF),
            pltpu.VMEM((3, R, LANES), BF),
            pltpu.VMEM((R, LANES), BF),
            pltpu.VMEM((16, R, LANES), BF),
            pltpu.VMEM((8, PIECE_ROWS, PIECE_PAD), BF),
            pltpu.VMEM((PIECE_PAD, 16 * R), BF),
            pltpu.VMEM((8 * R, 8 * PIECE_ROWS), BF),
            pltpu.VMEM((8 * R, 16 * R), BF),
            pltpu.VMEM((8, R, LANES), BF),
            pltpu.VMEM((7, R, LANES), BF),
            pltpu.VMEM((R, LANES), F32),
            pltpu.VMEM((CHUNKS * AUX * MU, R), BF),
            pltpu.VMEM((CHUNKS * AUX * MU, LANES), F32),
            pltpu.VMEM((CHUNKS * LANES, OCC), BF),
            dma((STEPS + 3,)),
            dma((3,)), dma((3,)),
            dma((7,)), dma((7,)),
            dma((3,)), dma((3,)),
            dma((15,)), dma((15,)),
            dma((7,)), dma((7,)),
        ],
        compiler_params=pltpu.CompilerParams(collective_id=0, has_side_effects=True, vmem_limit_bytes=24 * 1024 * 1024),
    )(*(pltpu.with_memory_space_constraint(a, pltpu.HBM) for a in (integrals, coefficients.T, screening, metric_factor)))
    gamma = pl.pallas_call(
        gamma_kernel,
        name="gamma",
        out_shape=jax.ShapeDtypeStruct((AUX * MU, NBF), BF),
        in_specs=[vmem, vmem, vmem],
        out_specs=hbm,
        scratch_shapes=[pltpu.VMEM((AUX * MU, NBF), BF), dma((GAMMA_STEPS,))],
        compiler_params=pltpu.CompilerParams(vmem_limit_bytes=16 * 1024 * 1024),
    )(fitted, coef_all, mask)
    return gamma.reshape(AUX, MU, NBF)


def solution(mesh):
    return jax.shard_map(
        on_device,
        mesh=mesh,
        in_specs=(P("aux", None, "occ"), P("occ", None), P(), P("aux", None)),
        out_specs=P("aux", "occ", None),
        check_vma=False,
    )
```

```python
import jax
import jax.numpy as jnp
from jax import lax
from jax.experimental import pallas as pl
from jax.experimental.pallas import tpu as pltpu
from jax.sharding import PartitionSpec as P

MESH = pl.DeviceIdType.MESH
BF = jnp.bfloat16
F32 = jnp.float32
TILE = 128

AUX = 18
ROWS = 32
MU = 8
OCC = 48
NU = 1536
NBF = 6144
LANES = 128
CHUNKS = 3
R = 56
PIECE = 16 * AUX
PIECE_PAD = 384
PIECE_ROWS = 24
STEPS = 3
STEP_AUX = AUX // STEPS
STEP_ROWS = STEP_AUX * ROWS
GAMMA_STEPS = 6
METRIC_ORDER = ((6, 4, 2), (7, 5, 3, 1))


def iota(shape, dim):
    return lax.broadcasted_iota(jnp.int32, shape, dim)


def one_hot(cond):
    return jnp.where(cond, 1.0, 0.0).astype(F32).astype(BF)


def nn(a, b):
    return jnp.dot(a, b, preferred_element_type=F32)


def nt(a, b):
    return lax.dot_general(a, b, (((1,), (1,)), ((), ())), preferred_element_type=F32)


def exchange_kernel(
    integrals, coef_t, screening, metric,
    fitted_out, coef_out, mask_out,
    ints, coef, coef_n, values, mets, scr, pieces, spread, parts, sends, recv1, half, halves, mrecv, columns, rows, mexp, fsend, recv3, fit, pick, lanes, fold,
    load_sem, coef_send, coef_recv, msend, mrecv_sem, fsend_sem, send1, recv1_sem, send2, recv2_sem, send3, recv3_sem,
):
    aux = lax.axis_index("aux")
    occ = lax.axis_index("occ")
    z, xh, y = aux // 8, (aux // 4) % 2, aux % 4
    xl, core = occ // 2, occ % 2
    upper = z % 2
    sign = 2 * upper - 1
    place = upper * 8 + xh * 4 + y

    def at_z(distance):
        other = lax.rem(z + distance + 16, 16)
        return {"aux": other * 8 + xh * 4 + y, "occ": occ}

    def mate(k):
        return lax.rem(xl + k // 2, 2) * 2 + lax.rem(core + k % 2, 2)

    def near(k, way):
        zp, xx, yy = lax.rem(upper + k // 8, 2), lax.rem(xh + (k // 4) % 2, 2), lax.rem(y + 4 + way * (k % 4), 4)
        return {"aux": (z - upper + zp) * 8 + xx * 4 + yy, "occ": occ}

    loads = [
        pltpu.make_async_copy(screening, scr, load_sem.at[0]),
        pltpu.make_async_copy(coef_t, coef, load_sem.at[1]),
    ]
    for j in range(STEPS):
        part = pl.ds(j * STEP_AUX, STEP_AUX)
        loads.append(pltpu.make_async_copy(integrals.at[part], ints.at[part], load_sem.at[2 + j]))
    loads.append(pltpu.make_async_copy(metric, mets, load_sem.at[2 + STEPS]))
    for copy in loads[:2] + loads[-1:] + loads[2:-1]:
        copy.start()

    barrier = pltpu.get_barrier_semaphore()
    for k in range(1, 4):
        pl.semaphore_signal(barrier, inc=1, device_id={"aux": aux, "occ": mate(k)}, device_id_type=MESH)
    for k in range(1, 16):
        pl.semaphore_signal(barrier, inc=1, device_id=near(k, -1), device_id_type=MESH)
    for d in range(1, 8):
        pl.semaphore_signal(barrier, inc=1, device_id=at_z(sign * d), device_id_type=MESH)
    for d in range(2, 8, 2):
        pl.semaphore_signal(barrier, inc=1, device_id=at_z(-sign * d), device_id_type=MESH)

    widen = one_hot(iota((OCC, CHUNKS * LANES), 0) == iota((OCC, CHUNKS * LANES), 1) % OCC)
    keep = (iota((ROWS, CHUNKS * LANES), 0) % MU) == (iota((ROWS, CHUNKS * LANES), 1) // OCC)
    keep = jnp.tile(jnp.where(keep, 1.0, 0.0).astype(F32), (AUX, 1))
    row = iota((4 * R, 1), 0)
    col = iota((1, AUX * ROWS), 1) // MU
    for c in range(CHUNKS):
        p = row % R - AUX * c
        wanted = jnp.where((p >= 0) & (p < AUX), p * 4 + row // R, -1)
        spread[:, c * AUX * ROWS:(c + 1) * AUX * ROWS] = one_hot(wanted == col)
    own_tile = one_hot(iota((48, NU), 0) == occ * (NU // TILE) + iota((48, NU), 1) // TILE)
    loads[0].wait()
    screen = scr[...].astype(F32).astype(BF)
    mask = nn(screen, own_tile).astype(BF)

    loads[-1].wait()
    pieces[...] = jnp.zeros_like(pieces)
    for k in range(8):
        pieces[k, 0:AUX, 0:PIECE] = mets[:, k * PIECE:(k + 1) * PIECE]
    mrecv[0] = pieces[z // 2]

    loads[1].wait()
    coef_n[...] = coef[...].T
    for j in range(STEPS):
        loads[2 + j].wait()
        block = ints[j * STEP_AUX:(j + 1) * STEP_AUX] * mask[None]
        values[j * STEP_ROWS:(j + 1) * STEP_ROWS, :] = nn(block.reshape(STEP_ROWS, NU), coef_n[...]).astype(BF)
    wide = (nn(values[...], widen) * keep).astype(BF)
    for c in range(CHUNKS):
        parts[c * AUX * ROWS:(c + 1) * AUX * ROWS, :] = wide[:, c * LANES:(c + 1) * LANES]
    sends[...] = nn(spread[...], parts[...]).astype(BF).reshape(4, R, LANES)

    pl.semaphore_wait(barrier, 28)

    first = []
    for k in (3, 2, 1):
        copy = pltpu.make_async_remote_copy(
            src_ref=sends.at[mate(k)], dst_ref=recv1.at[k - 1], send_sem=send1.at[k - 1], recv_sem=recv1_sem.at[k - 1],
            device_id={"aux": aux, "occ": mate(k)}, device_id_type=MESH)
        copy.start()
        first.append(copy)

    def metric_copy(d):
        step = sign * d if d % 2 else -sign * d
        other = lax.rem(z + step + 16, 16)
        return pltpu.make_async_remote_copy(
            src_ref=pieces.at[other // 2], dst_ref=mrecv.at[d], send_sem=msend.at[d - 1], recv_sem=mrecv_sem.at[d - 1],
            device_id=at_z(step), device_id_type=MESH)

    def onward_copy(d):
        return pltpu.make_async_remote_copy(
            src_ref=mrecv.at[d], dst_ref=mrecv.at[d], send_sem=fsend_sem.at[d - 1], recv_sem=mrecv_sem.at[d - 1],
            device_id={"aux": aux, "occ": mate(1)}, device_id_type=MESH)

    for turn in range(2):
        @pl.when(core == turn)
        def _():
            for d in METRIC_ORDER[turn]:
                metric_copy(d).start()
    for copy in first:
        copy.wait_recv()
    total = sends[occ].astype(F32) + recv1[0].astype(F32) + recv1[1].astype(F32) + recv1[2].astype(F32)
    half[...] = total.astype(BF)

    second = []
    for k in (14, 13, 15, 6, 10, 12, 5, 7, 9, 11, 2, 4, 1, 3, 8):
        copy = pltpu.make_async_remote_copy(
            src_ref=half, dst_ref=halves.at[place], send_sem=send2.at[k - 1], recv_sem=recv2_sem.at[k - 1],
            device_id=near(k, 1), device_id_type=MESH)
        copy.start()
        second.append(copy)
    halves[place] = half[...]

    own_nu = pl.ds(pl.multiple_of(occ * NU, NU), NU)
    to_core = pltpu.make_async_remote_copy(
        src_ref=coef_t, dst_ref=coef_out.at[:, own_nu], send_sem=coef_send.at[0], recv_sem=coef_recv.at[0],
        device_id={"aux": aux, "occ": mate(1)}, device_id_type=MESH)
    to_core.start()
    to_chip = pltpu.make_async_remote_copy(
        src_ref=coef_t, dst_ref=coef_out.at[:, own_nu], send_sem=coef_send.at[1], recv_sem=coef_recv.at[1],
        device_id={"aux": aux, "occ": mate(2)}, device_id_type=MESH)
    to_chip.start()
    own_coef = pltpu.make_async_copy(coef, coef_out.at[:, own_nu], load_sem.at[0])
    own_coef.start()

    c_of_col = iota((PIECE_PAD, 16 * R), 1) % R
    source = (iota((PIECE_PAD, 16 * R), 1) // R) * AUX + c_of_col % AUX
    columns[...] = one_hot((iota((PIECE_PAD, 16 * R), 0) == source) & (c_of_col < CHUNKS * AUX))
    r_of_row = iota((8 * R, 1), 0) % R
    source = jnp.where(r_of_row < CHUNKS * AUX, (iota((8 * R, 1), 0) // R) * PIECE_ROWS + r_of_row % AUX, -1)
    rows[...] = one_hot(source == iota((1, 8 * PIECE_ROWS), 1))
    row = iota((AUX * MU, 1), 0)
    for c in range(CHUNKS):
        pick[c * AUX * MU:(c + 1) * AUX * MU, :] = one_hot(iota((1, R), 1) == row // MU + c * AUX)
        lanes[c * AUX * MU:(c + 1) * AUX * MU, :] = jnp.where(
            (iota((1, LANES), 1) + c * LANES) // OCC == row % MU, 1.0, 0.0).astype(F32)
    fold[...] = one_hot(iota((CHUNKS * LANES, OCC), 0) % OCC == iota((CHUNKS * LANES, OCC), 1))
    own_rows = one_hot(iota((16, ROWS), 1) == occ * MU + iota((16, ROWS), 0) % MU)
    own_screen = nn(own_rows, screen).astype(BF)
    for k in range(4):
        tile = one_hot(iota((48, NU), 0) == k * (NU // TILE) + iota((48, NU), 1) // TILE)
        mask_out[:, k * NU:(k + 1) * NU] = nn(own_screen, tile)[0:MU]

    for turn in range(2):
        @pl.when(core == turn)
        def _():
            for d in METRIC_ORDER[turn][::-1]:
                metric_copy(d).wait_recv()
                onward_copy(d).start()
            for d in METRIC_ORDER[1 - turn][::-1]:
                metric_copy(d).wait_recv()
    wide_metric = nn(mrecv[...].reshape(8 * PIECE_ROWS, PIECE_PAD), columns[...]).astype(BF)
    same = ((iota((8 * R, 1), 0) % R) // AUX) == ((iota((1, 16 * R), 1) % R) // AUX)
    mexp[...] = jnp.where(same, nn(rows[...], wide_metric), 0.0).astype(BF)

    for copy in second:
        copy.wait_recv()
    partial = nn(mexp[...], halves[...].reshape(16 * R, LANES)).reshape(8, R, LANES)
    fsend[...] = partial.astype(BF)

    third = []
    for d in (7, 6, 5, 4, 3, 2, 1):
        copy = pltpu.make_async_remote_copy(
            src_ref=fsend.at[d], dst_ref=recv3.at[d - 1], send_sem=send3.at[d - 1], recv_sem=recv3_sem.at[d - 1],
            device_id=at_z(sign * d), device_id_type=MESH)
        copy.start()
        third.append(copy)
    fit[...] = partial[0]

    to_chip.wait_recv()
    chip_nu = pl.ds(pl.multiple_of(mate(2) * NU, NU), NU)
    onward = pltpu.make_async_remote_copy(
        src_ref=coef_out.at[:, chip_nu], dst_ref=coef_out.at[:, chip_nu], send_sem=coef_send.at[2], recv_sem=coef_recv.at[2],
        device_id={"aux": aux, "occ": mate(1)}, device_id_type=MESH)
    onward.start()

    total = fit[...]
    for d in range(1, 8):
        third[7 - d].wait_recv()
        total = total + recv3[d - 1].astype(F32)

    value = (nn(pick[...], total.astype(BF)) * lanes[...]).astype(BF)
    value = jnp.concatenate([value[c * AUX * MU:(c + 1) * AUX * MU] for c in range(CHUNKS)], axis=1)
    fitted_out[...] = nn(value, fold[...]).astype(BF)

    own_coef.wait()
    to_core.wait_recv()
    onward.wait_recv()
    for turn in range(2):
        @pl.when(core == turn)
        def _():
            for d in METRIC_ORDER[turn]:
                metric_copy(d).wait_send()
                onward_copy(d).wait_send()
    for copy in first + second + third + [to_core, to_chip, onward]:
        copy.wait_send()


def gamma_kernel(fitted, coef, mask, out, buffer, sems):
    width = NBF // sems.shape[0]
    copies = []
    for k in range(sems.shape[0]):
        part = pl.ds(k * width, width)
        product = nn(fitted[...], coef[:, k * width:(k + 1) * width])
        scaled = product.reshape(AUX, MU, width) * mask[:, k * width:(k + 1) * width][None]
        buffer[:, k * width:(k + 1) * width] = scaled.reshape(AUX * MU, width).astype(BF)
        copies.append(pltpu.make_async_copy(buffer.at[:, part], out.at[:, part], sems.at[k]))
        copies[-1].start()
    for copy in copies:
        copy.wait()


def on_device(integrals, coefficients, screening, metric_factor):
    hbm = pl.BlockSpec(memory_space=pltpu.HBM)
    free = pl.BlockSpec(memory_space=pl.ANY)
    vmem = pl.BlockSpec(memory_space=pltpu.VMEM)
    dma = pltpu.SemaphoreType.DMA
    fitted, coef_all, mask = pl.pallas_call(
        exchange_kernel,
        name="exchange",
        out_shape=(
            jax.ShapeDtypeStruct((AUX * MU, OCC), BF),
            jax.ShapeDtypeStruct((OCC, NBF), BF),
            jax.ShapeDtypeStruct((MU, NBF), F32),
        ),
        in_specs=[hbm, hbm, hbm, hbm],
        out_specs=(vmem, free, vmem),
        scratch_shapes=[
            pltpu.VMEM((AUX, ROWS, NU), BF),
            pltpu.VMEM((OCC, NU), BF),
            pltpu.VMEM((NU, OCC), BF),
            pltpu.VMEM((AUX * ROWS, OCC), BF),
            pltpu.VMEM((AUX, 2304), BF),
            pltpu.VMEM((ROWS, 48), jnp.int32),
            pltpu.VMEM((8, PIECE_ROWS, PIECE_PAD), BF),
            pltpu.VMEM((4 * R, CHUNKS * AUX * ROWS), BF),
            pltpu.VMEM((CHUNKS * AUX * ROWS, LANES), BF),
            pltpu.VMEM((4, R, LANES), BF),
            pltpu.VMEM((3, R, LANES), BF),
            pltpu.VMEM((R, LANES), BF),
            pltpu.VMEM((16, R, LANES), BF),
            pltpu.VMEM((8, PIECE_ROWS, PIECE_PAD), BF),
            pltpu.VMEM((PIECE_PAD, 16 * R), BF),
            pltpu.VMEM((8 * R, 8 * PIECE_ROWS), BF),
            pltpu.VMEM((8 * R, 16 * R), BF),
            pltpu.VMEM((8, R, LANES), BF),
            pltpu.VMEM((7, R, LANES), BF),
            pltpu.VMEM((R, LANES), F32),
            pltpu.VMEM((CHUNKS * AUX * MU, R), BF),
            pltpu.VMEM((CHUNKS * AUX * MU, LANES), F32),
            pltpu.VMEM((CHUNKS * LANES, OCC), BF),
            dma((STEPS + 3,)),
            dma((3,)), dma((3,)),
            dma((7,)), dma((7,)), dma((7,)),
            dma((3,)), dma((3,)),
            dma((15,)), dma((15,)),
            dma((7,)), dma((7,)),
        ],
        compiler_params=pltpu.CompilerParams(collective_id=0, has_side_effects=True, vmem_limit_bytes=24 * 1024 * 1024),
    )(*(pltpu.with_memory_space_constraint(a, pltpu.HBM) for a in (integrals, coefficients.T, screening, metric_factor)))
    gamma = pl.pallas_call(
        gamma_kernel,
        name="gamma",
        out_shape=jax.ShapeDtypeStruct((AUX * MU, NBF), BF),
        in_specs=[vmem, vmem, vmem],
        out_specs=hbm,
        scratch_shapes=[pltpu.VMEM((AUX * MU, NBF), BF), dma((GAMMA_STEPS,))],
        compiler_params=pltpu.CompilerParams(vmem_limit_bytes=16 * 1024 * 1024),
    )(fitted, coef_all, mask)
    return gamma.reshape(AUX, MU, NBF)


def solution(mesh):
    return jax.shard_map(
        on_device,
        mesh=mesh,
        in_specs=(P("aux", None, "occ"), P("occ", None), P(), P("aux", None)),
        out_specs=P("aux", "occ", None),
        check_vma=False,
    )
```

```python
import jax
import jax.numpy as jnp
from jax import lax
from jax.experimental import pallas as pl
from jax.experimental.pallas import tpu as pltpu
from jax.sharding import PartitionSpec as P

MESH = pl.DeviceIdType.MESH
BF = jnp.bfloat16
F32 = jnp.float32
TILE = 128

AUX = 18
ROWS = 32
MU = 8
OCC = 48
NU = 1536
NBF = 6144
LANES = 128
CHUNKS = 3
R = 56
PIECE = 16 * AUX
PIECE_PAD = 384
PIECE_ROWS = 24
HALF = 16
GAMMA_STEPS = 6
METRIC_ORDER = ((6, 4, 2), (7, 5, 3, 1))


def iota(shape, dim):
    return lax.broadcasted_iota(jnp.int32, shape, dim)


def one_hot(cond):
    return jnp.where(cond, 1.0, 0.0).astype(F32).astype(BF)


def nn(a, b):
    return jnp.dot(a, b, preferred_element_type=F32)


def nt(a, b):
    return lax.dot_general(a, b, (((1,), (1,)), ((), ())), preferred_element_type=F32)


def exchange_kernel(
    integrals, coef_t, screening, metric,
    fitted_out, coef_out, mask_out,
    ints, coef, coef_n, mets, scr, pieces, spread, sends, kept, recv1, half, halves, mrecv, columns, rows, mexp, fsend, recv3, fit, pick, lanes, fold,
    load_sem, coef_send, coef_recv, msend, mrecv_sem, fsend_sem, send1, recv1_sem, send2, recv2_sem, send3, recv3_sem,
):
    aux = lax.axis_index("aux")
    occ = lax.axis_index("occ")
    z, xh, y = aux // 8, (aux // 4) % 2, aux % 4
    xl, core = occ // 2, occ % 2
    upper = z % 2
    sign = 2 * upper - 1
    place = upper * 8 + xh * 4 + y

    def at_z(distance):
        other = lax.rem(z + distance + 16, 16)
        return {"aux": other * 8 + xh * 4 + y, "occ": occ}

    def mate(k):
        return lax.rem(xl + k // 2, 2) * 2 + lax.rem(core + k % 2, 2)

    def near(k, way):
        zp, xx, yy = lax.rem(upper + k // 8, 2), lax.rem(xh + (k // 4) % 2, 2), lax.rem(y + 4 + way * (k % 4), 4)
        return {"aux": (z - upper + zp) * 8 + xx * 4 + yy, "occ": occ}

    loads = [
        pltpu.make_async_copy(screening, scr, load_sem.at[0]),
        pltpu.make_async_copy(coef_t, coef, load_sem.at[1]),
    ]
    for j in range(2):
        other_half = pl.ds(pl.multiple_of(lax.rem(xl + 1 + j, 2) * HALF, HALF), HALF)
        loads.append(pltpu.make_async_copy(integrals.at[:, other_half], ints.at[j], load_sem.at[2 + j]))
    loads.append(pltpu.make_async_copy(metric, mets, load_sem.at[4]))
    for copy in loads[:2] + loads[-1:] + loads[2:-1]:
        copy.start()

    barrier = pltpu.get_barrier_semaphore()
    for k in range(1, 4):
        pl.semaphore_signal(barrier, inc=1, device_id={"aux": aux, "occ": mate(k)}, device_id_type=MESH)
    for k in range(1, 16):
        pl.semaphore_signal(barrier, inc=1, device_id=near(k, -1), device_id_type=MESH)
    for d in range(1, 8):
        pl.semaphore_signal(barrier, inc=1, device_id=at_z(sign * d), device_id_type=MESH)
    for d in range(2, 8, 2):
        pl.semaphore_signal(barrier, inc=1, device_id=at_z(-sign * d), device_id_type=MESH)

    widen = one_hot(iota((OCC, CHUNKS * LANES), 0) == iota((OCC, CHUNKS * LANES), 1) % OCC)
    keep = (iota((HALF, CHUNKS * LANES), 0) % MU) == (iota((HALF, CHUNKS * LANES), 1) // OCC)
    keep = jnp.tile(jnp.where(keep, 1.0, 0.0).astype(F32), (AUX, 1))
    row = iota((2 * R, 1), 0)
    col = iota((1, AUX * HALF), 1) // MU
    for c in range(CHUNKS):
        p = row % R - AUX * c
        wanted = jnp.where((p >= 0) & (p < AUX), p * 2 + row // R, -1)
        spread[:, c * AUX * HALF:(c + 1) * AUX * HALF] = one_hot(wanted == col)
    turned = lax.rem(iota((ROWS, ROWS), 0) + (xl + 1) * HALF, ROWS)
    turned = one_hot(turned == iota((ROWS, ROWS), 1))
    own_tile = one_hot(iota((48, NU), 0) == occ * (NU // TILE) + iota((48, NU), 1) // TILE)
    loads[0].wait()
    screen = scr[...].astype(F32).astype(BF)
    mask = nn(nn(turned, screen).astype(BF), own_tile).astype(BF)

    loads[-1].wait()
    pieces[...] = jnp.zeros_like(pieces)
    for k in range(8):
        pieces[k, 0:AUX, 0:PIECE] = mets[:, k * PIECE:(k + 1) * PIECE]
    mrecv[0] = pieces[z // 2]

    def transform(j):
        loads[2 + j].wait()
        block = ints[j] * mask[j * HALF:(j + 1) * HALF][None]
        value = nn(block.reshape(AUX * HALF, NU), coef_n[...]).astype(BF)
        wide = (nn(value, widen) * keep).astype(BF)
        stacked = jnp.concatenate([wide[:, c * LANES:(c + 1) * LANES] for c in range(CHUNKS)], axis=0)
        return nn(spread[...], stacked).reshape(2, R, LANES)

    def send_partial(k):
        copy = pltpu.make_async_remote_copy(
            src_ref=sends.at[1 - k // 2, lax.rem(core + k % 2, 2)], dst_ref=recv1.at[k - 1],
            send_sem=send1.at[k - 1], recv_sem=recv1_sem.at[k - 1],
            device_id={"aux": aux, "occ": mate(k)}, device_id_type=MESH)
        copy.start()
        return copy

    loads[1].wait()
    coef_n[...] = coef[...].T
    sends[0] = transform(0).astype(BF)
    pl.semaphore_wait(barrier, 28)

    first = [send_partial(3), send_partial(2)]
    def metric_copy(d):
        step = sign * d if d % 2 else -sign * d
        other = lax.rem(z + step + 16, 16)
        return pltpu.make_async_remote_copy(
            src_ref=pieces.at[other // 2], dst_ref=mrecv.at[d], send_sem=msend.at[d - 1], recv_sem=mrecv_sem.at[d - 1],
            device_id=at_z(step), device_id_type=MESH)

    def onward_copy(d):
        return pltpu.make_async_remote_copy(
            src_ref=mrecv.at[d], dst_ref=mrecv.at[d], send_sem=fsend_sem.at[d - 1], recv_sem=mrecv_sem.at[d - 1],
            device_id={"aux": aux, "occ": mate(1)}, device_id_type=MESH)

    for turn in range(2):
        @pl.when(core == turn)
        def _():
            for d in METRIC_ORDER[turn]:
                metric_copy(d).start()
    own = transform(1)
    sends[1] = own.astype(BF)
    first.append(send_partial(1))
    kept[...] = own
    total = kept[core]
    for copy, k in zip(first[::-1], (1, 2, 3)):
        copy.wait_recv()
        total = total + recv1[k - 1].astype(F32)
    half[...] = total.astype(BF)

    second = []
    for k in (14, 13, 15, 6, 10, 12, 5, 7, 9, 11, 2, 4, 1, 3, 8):
        copy = pltpu.make_async_remote_copy(
            src_ref=half, dst_ref=halves.at[place], send_sem=send2.at[k - 1], recv_sem=recv2_sem.at[k - 1],
            device_id=near(k, 1), device_id_type=MESH)
        copy.start()
        second.append(copy)
    halves[place] = half[...]

    own_nu = pl.ds(pl.multiple_of(occ * NU, NU), NU)
    to_core = pltpu.make_async_remote_copy(
        src_ref=coef_t, dst_ref=coef_out.at[:, own_nu], send_sem=coef_send.at[0], recv_sem=coef_recv.at[0],
        device_id={"aux": aux, "occ": mate(1)}, device_id_type=MESH)
    to_core.start()
    to_chip = pltpu.make_async_remote_copy(
        src_ref=coef_t, dst_ref=coef_out.at[:, own_nu], send_sem=coef_send.at[1], recv_sem=coef_recv.at[1],
        device_id={"aux": aux, "occ": mate(2)}, device_id_type=MESH)
    to_chip.start()
    own_coef = pltpu.make_async_copy(coef, coef_out.at[:, own_nu], load_sem.at[0])
    own_coef.start()

    c_of_col = iota((PIECE_PAD, 16 * R), 1) % R
    source = (iota((PIECE_PAD, 16 * R), 1) // R) * AUX + c_of_col % AUX
    columns[...] = one_hot((iota((PIECE_PAD, 16 * R), 0) == source) & (c_of_col < CHUNKS * AUX))
    r_of_row = iota((8 * R, 1), 0) % R
    source = jnp.where(r_of_row < CHUNKS * AUX, (iota((8 * R, 1), 0) // R) * PIECE_ROWS + r_of_row % AUX, -1)
    rows[...] = one_hot(source == iota((1, 8 * PIECE_ROWS), 1))
    row = iota((AUX * MU, 1), 0)
    for c in range(CHUNKS):
        pick[c * AUX * MU:(c + 1) * AUX * MU, :] = one_hot(iota((1, R), 1) == row // MU + c * AUX)
        lanes[c * AUX * MU:(c + 1) * AUX * MU, :] = jnp.where(
            (iota((1, LANES), 1) + c * LANES) // OCC == row % MU, 1.0, 0.0).astype(F32)
    fold[...] = one_hot(iota((CHUNKS * LANES, OCC), 0) % OCC == iota((CHUNKS * LANES, OCC), 1))
    own_rows = one_hot(iota((16, ROWS), 1) == occ * MU + iota((16, ROWS), 0) % MU)
    own_screen = nn(own_rows, screen).astype(BF)
    for k in range(4):
        tile = one_hot(iota((48, NU), 0) == k * (NU // TILE) + iota((48, NU), 1) // TILE)
        mask_out[:, k * NU:(k + 1) * NU] = nn(own_screen, tile)[0:MU]

    for turn in range(2):
        @pl.when(core == turn)
        def _():
            for d in METRIC_ORDER[turn][::-1]:
                metric_copy(d).wait_recv()
                onward_copy(d).start()
            for d in METRIC_ORDER[1 - turn][::-1]:
                metric_copy(d).wait_recv()
    wide_metric = nn(mrecv[...].reshape(8 * PIECE_ROWS, PIECE_PAD), columns[...]).astype(BF)
    same = ((iota((8 * R, 1), 0) % R) // AUX) == ((iota((1, 16 * R), 1) % R) // AUX)
    mexp[...] = jnp.where(same, nn(rows[...], wide_metric), 0.0).astype(BF)

    for copy in second:
        copy.wait_recv()
    gathered = halves[...].reshape(16 * R, LANES)
    third = []
    for part in ((7, 6, 5, 4), (3, 2, 1, 0)):
        partial = nn(mexp[part[-1] * R:(part[0] + 1) * R, :], gathered)
        for d in part:
            lo = (d - part[-1]) * R
            if d == 0:
                fit[...] = partial[lo:lo + R]
                continue
            fsend[d] = partial[lo:lo + R].astype(BF)
            copy = pltpu.make_async_remote_copy(
                src_ref=fsend.at[d], dst_ref=recv3.at[d - 1], send_sem=send3.at[d - 1], recv_sem=recv3_sem.at[d - 1],
                device_id=at_z(sign * d), device_id_type=MESH)
            copy.start()
            third.append(copy)

    to_chip.wait_recv()
    chip_nu = pl.ds(pl.multiple_of(mate(2) * NU, NU), NU)
    onward = pltpu.make_async_remote_copy(
        src_ref=coef_out.at[:, chip_nu], dst_ref=coef_out.at[:, chip_nu], send_sem=coef_send.at[2], recv_sem=coef_recv.at[2],
        device_id={"aux": aux, "occ": mate(1)}, device_id_type=MESH)
    onward.start()

    total = fit[...]
    for d in range(1, 8):
        third[7 - d].wait_recv()
        total = total + recv3[d - 1].astype(F32)

    value = (nn(pick[...], total.astype(BF)) * lanes[...]).astype(BF)
    value = jnp.concatenate([value[c * AUX * MU:(c + 1) * AUX * MU] for c in range(CHUNKS)], axis=1)
    fitted_out[...] = nn(value, fold[...]).astype(BF)

    own_coef.wait()
    to_core.wait_recv()
    onward.wait_recv()
    for turn in range(2):
        @pl.when(core == turn)
        def _():
            for d in METRIC_ORDER[turn]:
                metric_copy(d).wait_send()
                onward_copy(d).wait_send()
    for copy in first + second + third + [to_core, to_chip, onward]:
        copy.wait_send()


def gamma_kernel(fitted, coef, mask, out, buffer, sems):
    width = NBF // sems.shape[0]
    copies = []
    for k in range(sems.shape[0]):
        part = pl.ds(k * width, width)
        product = nn(fitted[...], coef[:, k * width:(k + 1) * width])
        scaled = product.reshape(AUX, MU, width) * mask[:, k * width:(k + 1) * width][None]
        buffer[:, k * width:(k + 1) * width] = scaled.reshape(AUX * MU, width).astype(BF)
        copies.append(pltpu.make_async_copy(buffer.at[:, part], out.at[:, part], sems.at[k]))
        copies[-1].start()
    for copy in copies:
        copy.wait()


def on_device(integrals, coefficients, screening, metric_factor):
    hbm = pl.BlockSpec(memory_space=pltpu.HBM)
    free = pl.BlockSpec(memory_space=pl.ANY)
    vmem = pl.BlockSpec(memory_space=pltpu.VMEM)
    dma = pltpu.SemaphoreType.DMA
    fitted, coef_all, mask = pl.pallas_call(
        exchange_kernel,
        name="exchange",
        out_shape=(
            jax.ShapeDtypeStruct((AUX * MU, OCC), BF),
            jax.ShapeDtypeStruct((OCC, NBF), BF),
            jax.ShapeDtypeStruct((MU, NBF), F32),
        ),
        in_specs=[hbm, hbm, hbm, hbm],
        out_specs=(vmem, free, vmem),
        scratch_shapes=[
            pltpu.VMEM((2, AUX, HALF, NU), BF),
            pltpu.VMEM((OCC, NU), BF),
            pltpu.VMEM((NU, OCC), BF),
            pltpu.VMEM((AUX, 2304), BF),
            pltpu.VMEM((ROWS, 48), jnp.int32),
            pltpu.VMEM((8, PIECE_ROWS, PIECE_PAD), BF),
            pltpu.VMEM((2 * R, CHUNKS * AUX * HALF), BF),
            pltpu.VMEM((2, 2, R, LANES), BF),
            pltpu.VMEM((2, R, LANES), F32),
            pltpu.VMEM((3, R, LANES), BF),
            pltpu.VMEM((R, LANES), BF),
            pltpu.VMEM((16, R, LANES), BF),
            pltpu.VMEM((8, PIECE_ROWS, PIECE_PAD), BF),
            pltpu.VMEM((PIECE_PAD, 16 * R), BF),
            pltpu.VMEM((8 * R, 8 * PIECE_ROWS), BF),
            pltpu.VMEM((8 * R, 16 * R), BF),
            pltpu.VMEM((8, R, LANES), BF),
            pltpu.VMEM((7, R, LANES), BF),
            pltpu.VMEM((R, LANES), F32),
            pltpu.VMEM((CHUNKS * AUX * MU, R), BF),
            pltpu.VMEM((CHUNKS * AUX * MU, LANES), F32),
            pltpu.VMEM((CHUNKS * LANES, OCC), BF),
            dma((5,)),
            dma((3,)), dma((3,)),
            dma((7,)), dma((7,)), dma((7,)),
            dma((3,)), dma((3,)),
            dma((15,)), dma((15,)),
            dma((7,)), dma((7,)),
        ],
        compiler_params=pltpu.CompilerParams(collective_id=0, has_side_effects=True, vmem_limit_bytes=24 * 1024 * 1024),
    )(*(pltpu.with_memory_space_constraint(a, pltpu.HBM) for a in (integrals, coefficients.T, screening, metric_factor)))
    gamma = pl.pallas_call(
        gamma_kernel,
        name="gamma",
        out_shape=jax.ShapeDtypeStruct((AUX * MU, NBF), BF),
        in_specs=[vmem, vmem, vmem],
        out_specs=hbm,
        scratch_shapes=[pltpu.VMEM((AUX * MU, NBF), BF), dma((GAMMA_STEPS,))],
        compiler_params=pltpu.CompilerParams(vmem_limit_bytes=16 * 1024 * 1024),
    )(fitted, coef_all, mask)
    return gamma.reshape(AUX, MU, NBF)


def solution(mesh):
    return jax.shard_map(
        on_device,
        mesh=mesh,
        in_specs=(P("aux", None, "occ"), P("occ", None), P(), P("aux", None)),
        out_specs=P("aux", "occ", None),
        check_vma=False,
    )
```

```python
import jax
import jax.numpy as jnp
from jax import lax
from jax.experimental import pallas as pl
from jax.experimental.pallas import tpu as pltpu
from jax.sharding import PartitionSpec as P

MESH = pl.DeviceIdType.MESH
BF = jnp.bfloat16
F32 = jnp.float32
TILE = 128

AUX = 18
ROWS = 32
MU = 8
OCC = 48
NU = 1536
NBF = 6144
LANES = 128
CHUNKS = 3
R = 56
PIECE = 16 * AUX
PIECE_PAD = 384
PIECE_ROWS = 24
HALF = 16
GAMMA_STEPS = 6
METRIC_ORDER = ((7, 4, 3), (6, 5, 2, 1))


def iota(shape, dim):
    return lax.broadcasted_iota(jnp.int32, shape, dim)


def one_hot(cond):
    return jnp.where(cond, 1.0, 0.0).astype(F32).astype(BF)


def nn(a, b):
    return jnp.dot(a, b, preferred_element_type=F32)


def nt(a, b):
    return lax.dot_general(a, b, (((1,), (1,)), ((), ())), preferred_element_type=F32)


def exchange_kernel(
    integrals, coef_t, screening, metric,
    fitted_out, coef_out, mask_out,
    ints, coef, coef_n, mets, scr, pieces, spread, sends, kept, recv1, half, halves, mrecv, columns, rows, mexp, fsend, recv3, fit, pick, lanes, fold,
    load_sem, coef_send, coef_recv, msend, mrecv_sem, fsend_sem, send1, recv1_sem, send2, recv2_sem, send3, recv3_sem,
):
    aux = lax.axis_index("aux")
    occ = lax.axis_index("occ")
    z, xh, y = aux // 8, (aux // 4) % 2, aux % 4
    xl, core = occ // 2, occ % 2
    upper = z % 2
    sign = 2 * upper - 1
    place = upper * 8 + xh * 4 + y

    def at_z(distance):
        other = lax.rem(z + distance + 16, 16)
        return {"aux": other * 8 + xh * 4 + y, "occ": occ}

    def mate(k):
        return lax.rem(xl + k // 2, 2) * 2 + lax.rem(core + k % 2, 2)

    def near(k, way):
        zp, xx, yy = lax.rem(upper + k // 8, 2), lax.rem(xh + (k // 4) % 2, 2), lax.rem(y + 4 + way * (k % 4), 4)
        return {"aux": (z - upper + zp) * 8 + xx * 4 + yy, "occ": occ}

    loads = [
        pltpu.make_async_copy(screening, scr, load_sem.at[0]),
        pltpu.make_async_copy(coef_t, coef, load_sem.at[1]),
    ]
    for j in range(2):
        other_half = pl.ds(pl.multiple_of(lax.rem(xl + 1 + j, 2) * HALF, HALF), HALF)
        loads.append(pltpu.make_async_copy(integrals.at[:, other_half], ints.at[j], load_sem.at[2 + j]))
    loads.append(pltpu.make_async_copy(metric, mets, load_sem.at[4]))
    for copy in loads[:2] + loads[-1:] + loads[2:-1]:
        copy.start()

    barrier = pltpu.get_barrier_semaphore()
    for k in range(1, 4):
        pl.semaphore_signal(barrier, inc=1, device_id={"aux": aux, "occ": mate(k)}, device_id_type=MESH)
    for k in range(1, 16):
        pl.semaphore_signal(barrier, inc=1, device_id=near(k, -1), device_id_type=MESH)
    for d in range(1, 8):
        pl.semaphore_signal(barrier, inc=1, device_id=at_z(sign * d), device_id_type=MESH)
    for d in range(2, 8, 2):
        pl.semaphore_signal(barrier, inc=1, device_id=at_z(-sign * d), device_id_type=MESH)

    widen = one_hot(iota((OCC, CHUNKS * LANES), 0) == iota((OCC, CHUNKS * LANES), 1) % OCC)
    keep = (iota((HALF, CHUNKS * LANES), 0) % MU) == (iota((HALF, CHUNKS * LANES), 1) // OCC)
    keep = jnp.tile(jnp.where(keep, 1.0, 0.0).astype(F32), (AUX, 1))
    row = iota((2 * R, 1), 0)
    col = iota((1, AUX * HALF), 1) // MU
    for c in range(CHUNKS):
        p = row % R - AUX * c
        wanted = jnp.where((p >= 0) & (p < AUX), p * 2 + row // R, -1)
        spread[:, c * AUX * HALF:(c + 1) * AUX * HALF] = one_hot(wanted == col)
    turned = lax.rem(iota((ROWS, ROWS), 0) + (xl + 1) * HALF, ROWS)
    turned = one_hot(turned == iota((ROWS, ROWS), 1))
    own_tile = one_hot(iota((48, NU), 0) == occ * (NU // TILE) + iota((48, NU), 1) // TILE)
    loads[0].wait()
    screen = scr[...].astype(F32).astype(BF)
    mask = nn(nn(turned, screen).astype(BF), own_tile).astype(BF)

    loads[-1].wait()
    pieces[...] = jnp.zeros_like(pieces)
    for k in range(8):
        pieces[k, 0:AUX, 0:PIECE] = mets[:, k * PIECE:(k + 1) * PIECE]
    mrecv[0] = pieces[z // 2]

    def transform(j):
        loads[2 + j].wait()
        block = ints[j] * mask[j * HALF:(j + 1) * HALF][None]
        value = nn(block.reshape(AUX * HALF, NU), coef_n[...]).astype(BF)
        wide = (nn(value, widen) * keep).astype(BF)
        stacked = jnp.concatenate([wide[:, c * LANES:(c + 1) * LANES] for c in range(CHUNKS)], axis=0)
        return nn(spread[...], stacked).reshape(2, R, LANES)

    def send_partial(k):
        copy = pltpu.make_async_remote_copy(
            src_ref=sends.at[1 - k // 2, lax.rem(core + k % 2, 2)], dst_ref=recv1.at[k - 1],
            send_sem=send1.at[k - 1], recv_sem=recv1_sem.at[k - 1],
            device_id={"aux": aux, "occ": mate(k)}, device_id_type=MESH)
        copy.start()
        return copy

    loads[1].wait()
    coef_n[...] = coef[...].T
    sends[0] = transform(0).astype(BF)
    pl.semaphore_wait(barrier, 28)

    first = [send_partial(3), send_partial(2)]
    def metric_copy(d):
        step = sign * d if d % 2 else -sign * d
        other = lax.rem(z + step + 16, 16)
        return pltpu.make_async_remote_copy(
            src_ref=pieces.at[other // 2], dst_ref=mrecv.at[d], send_sem=msend.at[d - 1], recv_sem=mrecv_sem.at[d - 1],
            device_id=at_z(step), device_id_type=MESH)

    def onward_copy(d):
        return pltpu.make_async_remote_copy(
            src_ref=mrecv.at[d], dst_ref=mrecv.at[d], send_sem=fsend_sem.at[d - 1], recv_sem=mrecv_sem.at[d - 1],
            device_id={"aux": aux, "occ": mate(1)}, device_id_type=MESH)

    for turn in range(2):
        @pl.when(core == turn)
        def _():
            for d in METRIC_ORDER[turn]:
                metric_copy(d).start()
    own = transform(1)
    sends[1] = own.astype(BF)
    first.append(send_partial(1))
    kept[...] = own
    total = kept[core]
    for copy, k in zip(first[::-1], (1, 2, 3)):
        copy.wait_recv()
        total = total + recv1[k - 1].astype(F32)
    half[...] = total.astype(BF)

    second = []
    for k in (14, 13, 15, 6, 10, 12, 5, 7, 9, 11, 2, 4, 1, 3, 8):
        copy = pltpu.make_async_remote_copy(
            src_ref=half, dst_ref=halves.at[place], send_sem=send2.at[k - 1], recv_sem=recv2_sem.at[k - 1],
            device_id=near(k, 1), device_id_type=MESH)
        copy.start()
        second.append(copy)
    halves[place] = half[...]

    own_nu = pl.ds(pl.multiple_of(occ * NU, NU), NU)
    to_core = pltpu.make_async_remote_copy(
        src_ref=coef_t, dst_ref=coef_out.at[:, own_nu], send_sem=coef_send.at[0], recv_sem=coef_recv.at[0],
        device_id={"aux": aux, "occ": mate(1)}, device_id_type=MESH)
    to_core.start()
    to_chip = pltpu.make_async_remote_copy(
        src_ref=coef_t, dst_ref=coef_out.at[:, own_nu], send_sem=coef_send.at[1], recv_sem=coef_recv.at[1],
        device_id={"aux": aux, "occ": mate(2)}, device_id_type=MESH)
    to_chip.start()
    own_coef = pltpu.make_async_copy(coef, coef_out.at[:, own_nu], load_sem.at[0])
    own_coef.start()

    c_of_col = iota((PIECE_PAD, 16 * R), 1) % R
    source = (iota((PIECE_PAD, 16 * R), 1) // R) * AUX + c_of_col % AUX
    columns[...] = one_hot((iota((PIECE_PAD, 16 * R), 0) == source) & (c_of_col < CHUNKS * AUX))
    r_of_row = iota((8 * R, 1), 0) % R
    source = jnp.where(r_of_row < CHUNKS * AUX, (iota((8 * R, 1), 0) // R) * PIECE_ROWS + r_of_row % AUX, -1)
    rows[...] = one_hot(source == iota((1, 8 * PIECE_ROWS), 1))
    row = iota((AUX * MU, 1), 0)
    for c in range(CHUNKS):
        pick[c * AUX * MU:(c + 1) * AUX * MU, :] = one_hot(iota((1, R), 1) == row // MU + c * AUX)
        lanes[c * AUX * MU:(c + 1) * AUX * MU, :] = jnp.where(
            (iota((1, LANES), 1) + c * LANES) // OCC == row % MU, 1.0, 0.0).astype(F32)
    fold[...] = one_hot(iota((CHUNKS * LANES, OCC), 0) % OCC == iota((CHUNKS * LANES, OCC), 1))
    own_rows = one_hot(iota((16, ROWS), 1) == occ * MU + iota((16, ROWS), 0) % MU)
    own_screen = nn(own_rows, screen).astype(BF)
    for k in range(4):
        tile = one_hot(iota((48, NU), 0) == k * (NU // TILE) + iota((48, NU), 1) // TILE)
        mask_out[:, k * NU:(k + 1) * NU] = nn(own_screen, tile)[0:MU]

    for turn in range(2):
        @pl.when(core == turn)
        def _():
            for d in METRIC_ORDER[turn][::-1]:
                metric_copy(d).wait_recv()
                onward_copy(d).start()
            for d in METRIC_ORDER[1 - turn][::-1]:
                metric_copy(d).wait_recv()
    wide_metric = nn(mrecv[...].reshape(8 * PIECE_ROWS, PIECE_PAD), columns[...]).astype(BF)
    same = ((iota((8 * R, 1), 0) % R) // AUX) == ((iota((1, 16 * R), 1) % R) // AUX)
    mexp[...] = jnp.where(same, nn(rows[...], wide_metric), 0.0).astype(BF)

    for copy in second:
        copy.wait_recv()
    gathered = halves[...].reshape(16 * R, LANES)
    third = []
    for part in ((7, 6, 5, 4), (3, 2, 1, 0)):
        partial = nn(mexp[part[-1] * R:(part[0] + 1) * R, :], gathered)
        for d in part:
            lo = (d - part[-1]) * R
            if d == 0:
                fit[...] = partial[lo:lo + R]
                continue
            fsend[d] = partial[lo:lo + R].astype(BF)
            copy = pltpu.make_async_remote_copy(
                src_ref=fsend.at[d], dst_ref=recv3.at[d - 1], send_sem=send3.at[d - 1], recv_sem=recv3_sem.at[d - 1],
                device_id=at_z(sign * d), device_id_type=MESH)
            copy.start()
            third.append(copy)

    to_chip.wait_recv()
    chip_nu = pl.ds(pl.multiple_of(mate(2) * NU, NU), NU)
    onward = pltpu.make_async_remote_copy(
        src_ref=coef_out.at[:, chip_nu], dst_ref=coef_out.at[:, chip_nu], send_sem=coef_send.at[2], recv_sem=coef_recv.at[2],
        device_id={"aux": aux, "occ": mate(1)}, device_id_type=MESH)
    onward.start()

    total = fit[...]
    for d in range(1, 8):
        third[7 - d].wait_recv()
        total = total + recv3[d - 1].astype(F32)

    value = (nn(pick[...], total.astype(BF)) * lanes[...]).astype(BF)
    value = jnp.concatenate([value[c * AUX * MU:(c + 1) * AUX * MU] for c in range(CHUNKS)], axis=1)
    fitted_out[...] = nn(value, fold[...]).astype(BF)

    own_coef.wait()
    to_core.wait_recv()
    onward.wait_recv()
    for turn in range(2):
        @pl.when(core == turn)
        def _():
            for d in METRIC_ORDER[turn]:
                metric_copy(d).wait_send()
                onward_copy(d).wait_send()
    for copy in first + second + third + [to_core, to_chip, onward]:
        copy.wait_send()


def gamma_kernel(fitted, coef, mask, out, buffer, sems):
    width = NBF // sems.shape[0]
    copies = []
    for k in range(sems.shape[0]):
        part = pl.ds(k * width, width)
        product = nn(fitted[...], coef[:, k * width:(k + 1) * width])
        scaled = product.reshape(AUX, MU, width) * mask[:, k * width:(k + 1) * width][None]
        buffer[:, k * width:(k + 1) * width] = scaled.reshape(AUX * MU, width).astype(BF)
        copies.append(pltpu.make_async_copy(buffer.at[:, part], out.at[:, part], sems.at[k]))
        copies[-1].start()
    for copy in copies:
        copy.wait()


def on_device(integrals, coefficients, screening, metric_factor):
    hbm = pl.BlockSpec(memory_space=pltpu.HBM)
    free = pl.BlockSpec(memory_space=pl.ANY)
    vmem = pl.BlockSpec(memory_space=pltpu.VMEM)
    dma = pltpu.SemaphoreType.DMA
    fitted, coef_all, mask = pl.pallas_call(
        exchange_kernel,
        name="exchange",
        out_shape=(
            jax.ShapeDtypeStruct((AUX * MU, OCC), BF),
            jax.ShapeDtypeStruct((OCC, NBF), BF),
            jax.ShapeDtypeStruct((MU, NBF), F32),
        ),
        in_specs=[hbm, hbm, hbm, hbm],
        out_specs=(vmem, free, vmem),
        scratch_shapes=[
            pltpu.VMEM((2, AUX, HALF, NU), BF),
            pltpu.VMEM((OCC, NU), BF),
            pltpu.VMEM((NU, OCC), BF),
            pltpu.VMEM((AUX, 2304), BF),
            pltpu.VMEM((ROWS, 48), jnp.int32),
            pltpu.VMEM((8, PIECE_ROWS, PIECE_PAD), BF),
            pltpu.VMEM((2 * R, CHUNKS * AUX * HALF), BF),
            pltpu.VMEM((2, 2, R, LANES), BF),
            pltpu.VMEM((2, R, LANES), F32),
            pltpu.VMEM((3, R, LANES), BF),
            pltpu.VMEM((R, LANES), BF),
            pltpu.VMEM((16, R, LANES), BF),
            pltpu.VMEM((8, PIECE_ROWS, PIECE_PAD), BF),
            pltpu.VMEM((PIECE_PAD, 16 * R), BF),
            pltpu.VMEM((8 * R, 8 * PIECE_ROWS), BF),
            pltpu.VMEM((8 * R, 16 * R), BF),
            pltpu.VMEM((8, R, LANES), BF),
            pltpu.VMEM((7, R, LANES), BF),
            pltpu.VMEM((R, LANES), F32),
            pltpu.VMEM((CHUNKS * AUX * MU, R), BF),
            pltpu.VMEM((CHUNKS * AUX * MU, LANES), F32),
            pltpu.VMEM((CHUNKS * LANES, OCC), BF),
            dma((5,)),
            dma((3,)), dma((3,)),
            dma((7,)), dma((7,)), dma((7,)),
            dma((3,)), dma((3,)),
            dma((15,)), dma((15,)),
            dma((7,)), dma((7,)),
        ],
        compiler_params=pltpu.CompilerParams(collective_id=0, has_side_effects=True, vmem_limit_bytes=24 * 1024 * 1024),
    )(*(pltpu.with_memory_space_constraint(a, pltpu.HBM) for a in (integrals, coefficients.T, screening, metric_factor)))
    gamma = pl.pallas_call(
        gamma_kernel,
        name="gamma",
        out_shape=jax.ShapeDtypeStruct((AUX * MU, NBF), BF),
        in_specs=[vmem, vmem, vmem],
        out_specs=hbm,
        scratch_shapes=[pltpu.VMEM((AUX * MU, NBF), BF), dma((GAMMA_STEPS,))],
        compiler_params=pltpu.CompilerParams(vmem_limit_bytes=16 * 1024 * 1024),
    )(fitted, coef_all, mask)
    return gamma.reshape(AUX, MU, NBF)


def solution(mesh):
    return jax.shard_map(
        on_device,
        mesh=mesh,
        in_specs=(P("aux", None, "occ"), P("occ", None), P(), P("aux", None)),
        out_specs=P("aux", "occ", None),
        check_vma=False,
    )
```
